768 devices in a mesh: rep: 16 (over y, core), grp: 48 (over x, z).
Axes of the slice: x: 4, y: 8, z: 12, core: 2. Of those that a mesh axis runs over, the one named last changes fastest.
Arguments:
- master_weight: float32 [96, 384, 2048], P('grp', 'rep'), may hold values from -0.3125 to 0.3125
- m_code: bfloat16 [96, 384, 2048], P('grp', 'rep'), may hold values from -1 to 1
- m_scale: float32 [96, 384, 16], P('grp', 'rep'), may hold values from 0.1 to 3
- v_code: bfloat16 [96, 384, 2048], P('grp', 'rep'), may hold values from 0.0099487305 to 1
- v_scale: float32 [96, 384, 16], P('grp', 'rep'), may hold values from 0.1 to 3
- placement: int32 [96], replicated, may hold values from 0 to 95, each once
- route: int32 [196608], P(('rep', 'grp')), may hold values from 0 to 95, as said below
- x_rows: bfloat16 [196608, 384], P(('rep', 'grp')), may hold values from -6 to 6
- y_cot: bfloat16 [196608, 2048], P(('rep', 'grp')), may hold values from -6 to 6
Outputs:
- y_rows: bfloat16 [196608, 2048], P(('rep', 'grp'))
- x_grad: bfloat16 [196608, 384], P(('rep', 'grp'))
- master_next: float32 [96, 384, 2048], P('grp', 'rep')
- m_code_next: bfloat16 [96, 384, 2048], P('grp', 'rep')
- m_scale_next: float32 [96, 384, 16], P('grp', 'rep')
- v_code_next: bfloat16 [96, 384, 2048], P('grp', 'rep')
- v_scale_next: float32 [96, 384, 16], P('grp', 'rep')
The draws below stay inside these ranges and needn't reach their ends.
Inputs may be any that keep to these rules, and one draw needn't show every extreme that they name: Each expert once; slot s of the weight and moment arrays holds the expert placement[s]. `route`: in the 256 rows of one device no expert appears more than 4 times, and one expert appears exactly 4 times in the rows of every device.
All inputs are finite; a program needn't handle non-finite values. Where the reference program divides by a largest or mean magnitude, that divisor is 1e-20 or more.
Results may differ from the reference program's by a relative error of at most 0.015.
Values may be sent and summed in bfloat16 or wider, within the bound.
A program may use at most 32 MiB of HBM per device.

```python
import math
import jax
import jax.numpy as jnp
from jax import lax

D = 2048
FF = 384
EXPERTS = 96
ROWS_DEV = 256
ROW_LIMIT = 4
ROWS_REP = 12288
ROWS_ALL = 196608
PER_EXPERT = 2048
BLOCK = 128
ADAM_STEP = 100
N_REP = 16
N_GRP = 48


def draw_route(key, part):
    block_count = ROWS_ALL // ROWS_DEV
    remaining_experts = EXPERTS - 1
    popular_random_key, boost_random_key, block_random_key = jax.random.split(jax.random.fold_in(key, 7), 3)
    hot_expert = jax.random.randint(popular_random_key, (), 0, EXPERTS)
    routing_boost = jnp.repeat(jax.random.randint(boost_random_key, (remaining_experts,), 0, 4) * 256, ROW_LIMIT)
    candidate_expert = jnp.arange(remaining_experts * ROW_LIMIT, dtype=jnp.int32)

    def one_block(block_key):
        key_noise, key_order = jax.random.split(block_key)
        random_jitter = jax.random.randint(key_noise, (remaining_experts * ROW_LIMIT,), 0, 1024)
        routing_score = (random_jitter + routing_boost) * 4096 + candidate_expert
        unused, picked = lax.top_k(routing_score, ROWS_DEV - ROW_LIMIT)
        chosen = (hot_expert + 1 + picked // ROW_LIMIT) % EXPERTS
        filled = jnp.concatenate([jnp.full((ROW_LIMIT,), hot_expert, jnp.int32), chosen.astype(jnp.int32)])
        order = jax.random.permutation(key_order, ROWS_DEV)
        return filled[order]
    block_keys = jax.random.split(block_random_key, block_count)
    return jax.vmap(one_block)(block_keys).reshape(-1).astype(jnp.int32)


def shard_levels(key, shape, cuts, least, top_value):
    def one(dim, shards_of):
        draws = jax.random.uniform(jax.random.fold_in(jax.random.fold_in(key, 6), dim), (shards_of,), jnp.float32, least / len(cuts), top_value / len(cuts))
        return jnp.repeat(jnp.exp(draws), shape[dim] // shards_of).reshape((-1,) + (1,) * (len(shape) - dim - 1))

    gain = one(*cuts[0])
    for cut in cuts[1:]:
        gain = gain * one(*cut)
    return gain


def normal_values(key, shape, scale, bound, cuts=(), kind=jnp.bfloat16):
    array = scale * jax.random.normal(key, shape, jnp.float32)
    if cuts:
        array = array * shard_levels(key, shape, cuts, -0.22, 0.18)
    return jnp.clip(array, -bound, bound).astype(kind)


def setup_inputs(seed: int = 0) -> dict:
    streams_of = jax.random.split(jax.random.key(seed), 10)
    master_weight = normal_values(streams_of[0], (EXPERTS, FF, D), FF ** -0.5, 0.3125, ((0, 48), (1, 16)), jnp.float32)
    m_code = jnp.clip(jax.random.uniform(streams_of[1], (EXPERTS, FF, D), jnp.float32, -1.0, 1.0) * shard_levels(streams_of[1], (EXPERTS, FF, D), ((0, 48), (1, 16)), -0.4, 0.0), -1.0, 1.0).astype(jnp.bfloat16)
    m_scale = jnp.clip(jnp.exp(math.log(3.0) - 3.4011974 * jax.random.uniform(streams_of[2], (EXPERTS, FF, D // BLOCK), jnp.float32) ** shard_levels(streams_of[2], (EXPERTS, FF, D // BLOCK), ((0, 48), (1, 16)), -0.2, 0.2)), 0.1, 3.0)
    v_code = jnp.clip(0.0099487305 + 0.99005127 * jax.random.uniform(streams_of[3], (EXPERTS, FF, D), jnp.float32) ** shard_levels(streams_of[3], (EXPERTS, FF, D), ((0, 48), (1, 16)), -0.2, 0.2), 0.0099487305, 1.0).astype(jnp.bfloat16)
    v_scale = jnp.clip(jnp.exp(math.log(3.0) - 3.4011974 * jax.random.uniform(streams_of[4], (EXPERTS, FF, D // BLOCK), jnp.float32) ** shard_levels(streams_of[4], (EXPERTS, FF, D // BLOCK), ((0, 48), (1, 16)), -0.2, 0.2)), 0.1, 3.0)
    placement = jax.random.permutation(streams_of[5], EXPERTS).astype(jnp.int32)
    route = draw_route(jax.random.fold_in(streams_of[9], 71), 0)
    x_rows = normal_values(streams_of[7], (ROWS_ALL, FF), 1.0, 6.0, ((0, 768),))
    y_cot = normal_values(streams_of[8], (ROWS_ALL, D), 1.0, 6.0, ((0, 768),))
    return dict(master_weight=master_weight, m_code=m_code, m_scale=m_scale, v_code=v_code, v_scale=v_scale, placement=placement, route=route, x_rows=x_rows, y_cot=y_cot)


beta_one = 0.9
beta_two = 0.95
learn_rate = 0.01

def adam_update(master_weight, grad, m_code, m_scale, v_code, v_scale):
    full_shape = master_weight.shape
    blocked = full_shape[:-1] + (full_shape[-1] // BLOCK, BLOCK)
    m_old = (m_code.astype(jnp.float32).reshape(blocked) * m_scale[..., None]).reshape(full_shape)
    v_old = (v_code.astype(jnp.float32).reshape(blocked) * v_scale[..., None]).reshape(full_shape)
    m_next = beta_one * m_old + (1.0 - beta_one) * grad
    v_next = beta_two * v_old + (1.0 - beta_two) * grad * grad
    corr_one = 1.0 - beta_one ** ADAM_STEP
    corr_two = 1.0 - beta_two ** ADAM_STEP
    step_size = m_next / corr_one / (jnp.sqrt(v_next / corr_two) + 1e-08)
    master_next = master_weight - learn_rate * step_size
    m_blocks = m_next.reshape(blocked)
    v_blocks = v_next.reshape(blocked)
    m_scale_next = lax.optimization_barrier(jnp.max(jnp.abs(m_blocks), axis=-1)) + 1e-06
    v_scale_next = lax.optimization_barrier(jnp.max(v_blocks, axis=-1)) + 1e-06
    m_code_next = (m_blocks / m_scale_next[..., None]).reshape(full_shape).astype(jnp.bfloat16)
    v_code_next = (v_blocks / v_scale_next[..., None]).reshape(full_shape).astype(jnp.bfloat16)
    return (master_next, m_code_next, m_scale_next, v_code_next, v_scale_next)

def reference(master_weight, m_code, m_scale, v_code, v_scale, placement, route, x_rows, y_cot):
    expert_ids = jnp.arange(EXPERTS, dtype=jnp.int32)
    slot_rows = N_GRP * ROW_LIMIT
    grad_factor = float(PER_EXPERT) ** (-0.5)
    weight_low = master_weight.astype(jnp.bfloat16)
    weight_full = lax.optimization_barrier(weight_low).astype(jnp.float32)
    sources = jnp.arange(N_GRP, dtype=jnp.int32)

    def replica(total, inputs):
        routes_here, x_here, g_here = inputs
        slot = lax.optimization_barrier(jnp.sum(jnp.where(placement[None, :] == routes_here[:, None], expert_ids[None, :], 0), axis=1)).astype(jnp.int32)
        slot_grid = slot.reshape(N_GRP, ROWS_DEV)
        slot_hot = (slot_grid[:, :, None] == expert_ids[None, None, :]).astype(jnp.int32)
        position = lax.optimization_barrier(jnp.sum(slot_hot * (jnp.cumsum(slot_hot, axis=1) - 1), axis=2)).astype(jnp.int32)
        target = (slot_grid * slot_rows + sources[:, None] * ROW_LIMIT + position).reshape(-1).astype(jnp.int32)
        buffer_x = jnp.zeros((EXPERTS * slot_rows, FF), jnp.float32).at[target].set(x_here.astype(jnp.float32))
        buffer_g = jnp.zeros((EXPERTS * slot_rows, D), jnp.float32).at[target].set(g_here.astype(jnp.float32))
        buffer_x = buffer_x.reshape(EXPERTS, slot_rows, FF)
        buffer_g = buffer_g.reshape(EXPERTS, slot_rows, D)
        out_y = jnp.einsum('esf,efd->esd', buffer_x, weight_full)
        out_dx = jnp.einsum('esd,efd->esf', buffer_g, weight_full)
        part_low = (jnp.einsum('esf,esd->efd', buffer_x, buffer_g) * grad_factor).astype(jnp.bfloat16)
        part_grad = lax.optimization_barrier(part_low).astype(jnp.float32)
        y_here = out_y.reshape(-1, D)[target].astype(jnp.bfloat16)
        dx_here = out_dx.reshape(-1, FF)[target].astype(jnp.bfloat16)
        return (total + part_grad, (y_here, dx_here))
    start_total = jnp.zeros((EXPERTS, FF, D), jnp.float32)
    grad, outputs = lax.scan(replica, start_total, (route.reshape(N_REP, ROWS_REP), x_rows.reshape(N_REP, ROWS_REP, FF), y_cot.reshape(N_REP, ROWS_REP, D)))
    y_rows = outputs[0].reshape(ROWS_ALL, D)
    x_grad = outputs[1].reshape(ROWS_ALL, FF)
    master_next, m_code_next, m_scale_next, v_code_next, v_scale_next = adam_update(master_weight, grad, m_code, m_scale, v_code, v_scale)
    return (y_rows, x_grad, master_next, m_code_next, m_scale_next, v_code_next, v_scale_next)
```

```python
import jax
import jax.numpy as jnp
from jax import lax
from jax.sharding import PartitionSpec as P

BLOCK = 128
ADAM_STEP = 100


beta_one = 0.9
beta_two = 0.95
learn_rate = 0.01


def adam_update(master_weight, grad, m_code, m_scale, v_code, v_scale):
    full_shape = master_weight.shape
    blocked = full_shape[:-1] + (full_shape[-1] // BLOCK, BLOCK)
    m_old = (m_code.astype(jnp.float32).reshape(blocked) * m_scale[..., None]).reshape(full_shape)
    v_old = (v_code.astype(jnp.float32).reshape(blocked) * v_scale[..., None]).reshape(full_shape)
    m_next = beta_one * m_old + (1.0 - beta_one) * grad
    v_next = beta_two * v_old + (1.0 - beta_two) * grad * grad
    corr_one = 1.0 - beta_one**ADAM_STEP
    corr_two = 1.0 - beta_two**ADAM_STEP
    step_size = m_next / corr_one / (jnp.sqrt(v_next / corr_two) + 1e-08)
    master_next = master_weight - learn_rate * step_size
    m_blocks = m_next.reshape(blocked)
    v_blocks = v_next.reshape(blocked)
    m_scale_next = jnp.max(jnp.abs(m_blocks), axis=-1) + 1e-06
    v_scale_next = jnp.max(v_blocks, axis=-1) + 1e-06
    m_code_next = (m_blocks / m_scale_next[..., None]).reshape(full_shape).astype(jnp.bfloat16)
    v_code_next = (v_blocks / v_scale_next[..., None]).reshape(full_shape).astype(jnp.bfloat16)
    return (master_next, m_code_next, m_scale_next, v_code_next, v_scale_next)


def per_device(master_weight, m_code, m_scale, v_code, v_scale, placement, route, x_rows, y_cot):
    local_count, slice_rows, model_width = master_weight.shape
    row_count, hidden_width = x_rows.shape
    expert_count = placement.shape[0]
    groups = lax.axis_size("grp")
    replicas = lax.axis_size("rep")
    grad_factor = float(row_count * groups * replicas // expert_count) ** (-0.5)
    capacity = max(2, (3 * row_count + 2 * expert_count - 1) // (2 * expert_count))
    block_rows = local_count * capacity
    slots = groups * block_rows
    weight_slice = lax.optimization_barrier(master_weight.astype(jnp.bfloat16))
    weight_rows = lax.all_gather(weight_slice, "rep", axis=1, tiled=True)
    expert_ids = lax.iota(jnp.int32, expert_count)
    route_hot = (route[:, None] == expert_ids[None, :]).astype(jnp.int32)
    position = jnp.sum(route_hot * (jnp.cumsum(route_hot, axis=0) - 1), axis=1)
    slot = jnp.sum(jnp.where(placement[None, :] == route[:, None], expert_ids[None, :], 0), axis=1)
    target = slot * capacity + position
    places = (target[:, None] == lax.iota(jnp.int32, slots)[None, :]).astype(jnp.bfloat16)
    rows = jnp.concatenate([x_rows, y_cot], axis=1)
    send = lax.dot_general(
        places, rows, (((0,), (0,)), ((), ())), preferred_element_type=jnp.float32
    ).astype(jnp.bfloat16)
    width = hidden_width + model_width
    recv = lax.all_to_all(
        send.reshape(groups, block_rows, width), "grp", split_axis=0, concat_axis=0, tiled=True
    ).reshape(slots, width)
    recv, weight_rows = lax.optimization_barrier((recv, weight_rows))
    member = lax.broadcasted_iota(jnp.int32, (slots, 1), 0) % block_rows // capacity
    local_x, local_g = recv[:, :hidden_width], recv[:, hidden_width:]
    wide_x = jnp.concatenate(
        [jnp.where(member == m, local_x, jnp.zeros_like(local_x)) for m in range(local_count)], axis=1
    )
    outer = lax.dot_general(
        wide_x, local_g, (((0,), (0,)), ((), ())), preferred_element_type=jnp.float32
    )
    part_grad = (outer * grad_factor).astype(jnp.bfloat16)
    part_grad = part_grad.reshape(local_count, hidden_width, model_width)
    grad = lax.psum_scatter(part_grad, "rep", scatter_dimension=1, tiled=True).astype(jnp.float32)
    weight_flat = weight_rows.reshape(local_count * hidden_width, model_width)
    y_total = jnp.dot(wide_x, weight_flat, preferred_element_type=jnp.float32)
    dx_wide = lax.dot_general(
        local_g, weight_flat, (((1,), (1,)), ((), ())), preferred_element_type=jnp.float32
    )
    dx_total = dx_wide[:, :hidden_width]
    for m in range(1, local_count):
        dx_total = jnp.where(
            member == m, dx_wide[:, m * hidden_width : (m + 1) * hidden_width], dx_total
        )
    back = jnp.concatenate([dx_total, y_total], axis=1).astype(jnp.bfloat16)
    home = lax.all_to_all(
        back.reshape(groups, block_rows, width), "grp", split_axis=0, concat_axis=0, tiled=True
    ).reshape(slots, width)
    y_rows = jnp.dot(places, home[:, hidden_width:], preferred_element_type=jnp.float32).astype(
        jnp.bfloat16
    )
    x_grad = jnp.dot(places, home[:, :hidden_width], preferred_element_type=jnp.float32).astype(
        jnp.bfloat16
    )
    return (y_rows, x_grad) + adam_update(master_weight, grad, m_code, m_scale, v_code, v_scale)


def solution(mesh):
    state = P("grp", "rep", None)
    rows = P(("rep", "grp"), None)
    return jax.shard_map(
        per_device,
        mesh=mesh,
        in_specs=(state, state, state, state, state, P(), P(("rep", "grp")), rows, rows),
        out_specs=(rows, rows, state, state, state, state, state),
        check_vma=False,
    )
```

```python
import jax
import jax.numpy as jnp
from jax import lax
from jax.experimental import pallas as pl
from jax.experimental.pallas import tpu as pltpu
from jax.sharding import PartitionSpec as P

BLOCK = 128
ADAM_STEP = 100
GRID_X = 4
GRID_Y = 8
GRID_Z = 12
HALF_Z = GRID_Z // 2
PEERS = 2 * GRID_X * HALF_Z
MESH = pl.DeviceIdType.MESH
TIE = 3
VMEM_LIMIT = 40 * 1024 * 1024


beta_one = 0.9
beta_two = 0.95
learn_rate = 0.01


def adam_update(master_weight, grad, m_code, m_scale, v_code, v_scale):
    full_shape = master_weight.shape
    blocked = full_shape[:-1] + (full_shape[-1] // BLOCK, BLOCK)
    m_old = (m_code.astype(jnp.float32).reshape(blocked) * m_scale[..., None]).reshape(full_shape)
    v_old = (v_code.astype(jnp.float32).reshape(blocked) * v_scale[..., None]).reshape(full_shape)
    m_next = beta_one * m_old + (1.0 - beta_one) * grad
    v_next = beta_two * v_old + (1.0 - beta_two) * grad * grad
    corr_one = 1.0 - beta_one**ADAM_STEP
    corr_two = 1.0 - beta_two**ADAM_STEP
    step_size = m_next / corr_one / (jnp.sqrt(v_next / corr_two) + 1e-08)
    master_next = master_weight - learn_rate * step_size
    m_blocks = m_next.reshape(blocked)
    v_blocks = v_next.reshape(blocked)
    m_scale_next = jnp.max(jnp.abs(m_blocks), axis=-1) + 1e-06
    v_scale_next = jnp.max(v_blocks, axis=-1) + 1e-06
    m_code_next = (m_blocks / m_scale_next[..., None]).reshape(full_shape).astype(jnp.bfloat16)
    v_code_next = (v_blocks / v_scale_next[..., None]).reshape(full_shape).astype(jnp.bfloat16)
    return (master_next, m_code_next, m_scale_next, v_code_next, v_scale_next)


def offset_of(d):
    return jnp.where(d < TIE, d, d - HALF_Z)


class Place:
    def __init__(self):
        rep, grp = lax.axis_index("rep"), lax.axis_index("grp")
        self.y, self.c = rep // 2, rep % 2
        self.x, self.z = grp // GRID_Z, grp % GRID_Z

    def device(self, y=0, c=0, x=0, z=0):
        rep = (self.y + y + GRID_Y) % GRID_Y * 2 + (self.c + c) % 2
        grp = (self.x + x) % GRID_X * GRID_Z + (self.z + z + GRID_Z) % GRID_Z
        return rep, grp

    def slot(self, c, x, d):
        return ((self.c + c) % 2 * GRID_X + (self.x + x) % GRID_X) * HALF_Z + d


def signal(device):
    pl.semaphore_signal(
        pltpu.get_barrier_semaphore(), inc=1, device_id=device, device_id_type=MESH
    )


def enter(place, sign):
    def greet(i, carry):
        d, c, x = i // (2 * GRID_X), i // GRID_X % 2, i % GRID_X

        @pl.when(i != 0)
        def _():
            signal(place.device(c=c, x=x, z=-sign * offset_of(d)))

        return carry

    signal(place.device(z=HALF_Z))
    signal(place.device(c=1, z=HALF_Z))
    signal(place.device(y=1))
    signal(place.device(y=-1))
    lax.fori_loop(0, PEERS, greet, 0)
    pl.semaphore_wait(pltpu.get_barrier_semaphore(), PEERS - 1 + 4)


def row_copy(place, source, target, send_sem, recv_sem, sign, c, x, d):
    there = place.slot(c, x, d)
    here = place.slot(0, 0, d)
    return pltpu.make_async_remote_copy(
        src_ref=source.at[there],
        dst_ref=target.at[here],
        send_sem=send_sem.at[there],
        recv_sem=recv_sem.at[here],
        device_id=place.device(c=c, x=x, z=sign * offset_of(d)),
        device_id_type=MESH,
    )


def rows_start(place, source, target, send_sem, recv_sem, sign):
    own = place.slot(0, 0, 0)
    pltpu.make_async_copy(source.at[own], target.at[own], recv_sem.at[own]).start()

    def step(i, carry):
        d, c, x = i // (2 * GRID_X), i // GRID_X % 2, i % GRID_X
        d = (d + 3) % HALF_Z

        @pl.when(jnp.logical_or(d != 0, i % (2 * GRID_X) != 0))
        def _():
            row_copy(place, source, target, send_sem, recv_sem, sign, c, x, d).start()

        return carry

    lax.fori_loop(0, PEERS, step, 0)


def rows_wait(place, source, target, send_sem, recv_sem, sign):
    own = place.slot(0, 0, 0)

    def step(i, carry):
        copy = pltpu.make_async_remote_copy(
            src_ref=source.at[i],
            dst_ref=target.at[i],
            send_sem=send_sem.at[i],
            recv_sem=recv_sem.at[i],
            device_id=place.device(y=1),
            device_id_type=MESH,
        )

        @pl.when(i != own)
        def _():
            copy.wait_send()
            copy.wait_recv()

        return carry

    lax.fori_loop(0, PEERS, step, 0)
    pltpu.make_async_copy(source.at[own], target.at[own], recv_sem.at[own]).wait()


def remote(source, target, send_sem, recv_sem, device):
    return pltpu.make_async_remote_copy(
        src_ref=source,
        dst_ref=target,
        send_sem=send_sem,
        recv_sem=recv_sem,
        device_id=device,
        device_id_type=MESH,
    )


def dispatch_kernel(
    rows_ref, slice_ref, recv_ref, full_ref,
    row_send, row_recv, first_send, first_recv, ring_send, ring_recv, local_sem,
):
    place = Place()
    y, c = place.y, place.c
    enter(place, 1)
    own = pltpu.make_async_copy(slice_ref.at[c], full_ref.at[0, y, c], local_sem)
    own.start()
    far = []
    for m in range(2):
        far.append(
            remote(
                slice_ref.at[(c + m) % 2], full_ref.at[1, y, c],
                first_send.at[1 + m], first_recv.at[1 + c], place.device(c=m, z=HALF_Z),
            )
        )
        far[m].start()
    near = remote(
        slice_ref.at[1 - c], full_ref.at[0, y, c],
        first_send.at[0], first_recv.at[0], place.device(c=1),
    )
    near.start()
    rows_start(place, rows_ref, recv_ref, row_send, row_recv, 1)
    pending = []
    for h in range(2):
        if h == 0:
            own.wait()
            near.wait()
        else:
            for m in range(2):
                remote(
                    slice_ref.at[m], full_ref.at[1, y, m],
                    first_send.at[1 + m], first_recv.at[1 + m], place.device(z=HALF_Z),
                ).wait()
        for step in range(4):
            arrived = []
            for way in range(2):
                sign = 1 - 2 * way
                origin = (y - sign * step + GRID_Y) % GRID_Y
                if step < 3:
                    block = full_ref.at[h, origin]
                else:
                    block = full_ref.at[h, origin, way]
                copy = remote(
                    block, block, ring_send.at[h, way, step], ring_recv.at[h, way, step],
                    place.device(y=sign),
                )
                copy.start()
                pending.append(copy)
                origin = (y - sign * (step + 1) + GRID_Y) % GRID_Y
                if step < 3:
                    block = full_ref.at[h, origin]
                else:
                    block = full_ref.at[h, origin, way]
                arrived.append(
                    remote(
                        block, block, ring_send.at[h, way, step], ring_recv.at[h, way, step],
                        place.device(y=sign),
                    )
                )
            for copy in arrived:
                copy.wait_recv()
    for copy in pending:
        copy.wait_send()
    rows_wait(place, rows_ref, recv_ref, row_send, row_recv, 1)


def return_kernel(
    rows_ref, part_ref, home_ref, grad_ref,
    hold, total, row_send, row_recv, ring_send, ring_recv, last_send, last_recv, local_sem,
):
    place = Place()
    y, c = place.y, place.c
    enter(place, -1)
    rows_start(place, rows_ref, home_ref, row_send, row_recv, -1)
    pending = []
    for h in (1, 0):
        for step in range(4):
            arrived = []
            for way in range(2):
                sign = 1 - 2 * way
                target = (y + sign * (4 - step) + GRID_Y) % GRID_Y
                if step == 0:
                    source, into = part_ref.at[h, target, way], hold.at[h, way, step, way]
                else:
                    held = hold.at[h, way, step - 1]
                    if step == 1:
                        held[way] = (
                            held[way].astype(jnp.float32)
                            + part_ref[h, target, way].astype(jnp.float32)
                        ).astype(jnp.bfloat16)
                        held[1 - way] = part_ref[h, target, 1 - way]
                    else:
                        held[...] = (
                            held[...].astype(jnp.float32)
                            + part_ref[h, target].astype(jnp.float32)
                        ).astype(jnp.bfloat16)
                    source, into = held, hold.at[h, way, step]
                copy = remote(
                    source, into, ring_send.at[h, way, step], ring_recv.at[h, way, step],
                    place.device(y=sign),
                )
                copy.start()
                pending.append(copy)
                arrived.append(copy)
            for copy in arrived:
                copy.wait_recv()
        total[h] = (
            part_ref[h, y].astype(jnp.float32)
            + hold[h, 0, 3].astype(jnp.float32)
            + hold[h, 1, 3].astype(jnp.float32)
        ).astype(jnp.bfloat16)
        if h == 1:
            far = []
            for m in range(2):
                far.append(
                    remote(
                        total.at[1, (c + m) % 2], grad_ref.at[c, 1],
                        last_send.at[1 + m], last_recv.at[1 + c], place.device(c=m, z=HALF_Z),
                    )
                )
                far[m].start()
        else:
            own = pltpu.make_async_copy(total.at[0, c], grad_ref.at[c, 0], local_sem)
            own.start()
            near = remote(
                total.at[0, 1 - c], grad_ref.at[c, 0],
                last_send.at[0], last_recv.at[0], place.device(c=1),
            )
            near.start()
    for copy in pending:
        copy.wait_send()
    own.wait()
    near.wait()
    for m in range(2):
        remote(
            total.at[1, m], grad_ref.at[m, 1],
            last_send.at[1 + m], last_recv.at[1 + m], place.device(z=HALF_Z),
        ).wait()
    rows_wait(place, rows_ref, home_ref, row_send, row_recv, -1)


VMEM = pl.BlockSpec(memory_space=pltpu.VMEM)
DMA = pltpu.SemaphoreType.DMA


def dispatch(rows, weight_slice):
    members, slice_rows, width = weight_slice.shape
    return pl.pallas_call(
        dispatch_kernel,
        out_shape=(
            jax.ShapeDtypeStruct(rows.shape, rows.dtype),
            jax.ShapeDtypeStruct((2, GRID_Y, 2, slice_rows, width), weight_slice.dtype),
        ),
        in_specs=[VMEM] * 2,
        out_specs=(VMEM, VMEM),
        scratch_shapes=[
            DMA((PEERS,)), DMA((PEERS,)), DMA((3,)), DMA((3,)),
            DMA((2, 2, 4)), DMA((2, 2, 4)), DMA(()),
        ],
        compiler_params=pltpu.CompilerParams(
            collective_id=0, has_side_effects=True, vmem_limit_bytes=VMEM_LIMIT
        ),
        name="dispatch",
    )(rows, weight_slice)


def give_back(rows, part):
    slice_rows, width = part.shape[-2:]
    return pl.pallas_call(
        return_kernel,
        out_shape=(
            jax.ShapeDtypeStruct(rows.shape, rows.dtype),
            jax.ShapeDtypeStruct((2, 2, slice_rows, width), part.dtype),
        ),
        in_specs=[VMEM] * 2,
        out_specs=(VMEM, VMEM),
        scratch_shapes=[
            pltpu.VMEM((2, 2, 4, 2, slice_rows, width), part.dtype),
            pltpu.VMEM((2, 2, slice_rows, width), part.dtype),
            DMA((PEERS,)), DMA((PEERS,)), DMA((2, 2, 4)), DMA((2, 2, 4)),
            DMA((3,)), DMA((3,)), DMA(()),
        ],
        compiler_params=pltpu.CompilerParams(
            collective_id=1, has_side_effects=True, vmem_limit_bytes=VMEM_LIMIT
        ),
        name="give_back",
    )(rows, part)


def per_device(master_weight, m_code, m_scale, v_code, v_scale, placement, route, x_rows, y_cot):
    members, slice_rows, model_width = master_weight.shape
    row_count, hidden_width = x_rows.shape
    expert_count = placement.shape[0]
    groups = lax.axis_size("grp")
    replicas = lax.axis_size("rep")
    grad_factor = float(row_count * groups * replicas // expert_count) ** (-0.5)
    capacity = max(2, (3 * row_count + 2 * expert_count - 1) // (2 * expert_count))
    block_rows = 2 * capacity
    slots = PEERS * block_rows
    weight_slice = master_weight.astype(jnp.bfloat16)
    expert_ids = lax.iota(jnp.int32, expert_count)
    route_hot = (route[:, None] == expert_ids[None, :]).astype(jnp.int32)
    position = jnp.sum(route_hot * (jnp.cumsum(route_hot, axis=0) - 1), axis=1)
    slot = jnp.sum(jnp.where(placement[None, :] == route[:, None], expert_ids[None, :], 0), axis=1)
    here_z = lax.axis_index("grp") % GRID_Z
    core, chip_x, chip_z = slot % members, slot // members // GRID_Z, slot // members % GRID_Z
    d = (chip_z - here_z + GRID_Z) % HALF_Z
    far = ((here_z + offset_of(d) + GRID_Z) % GRID_Z != chip_z).astype(jnp.int32)
    target = ((core * GRID_X + chip_x) * HALF_Z + d) * block_rows + far * capacity + position
    places = (target[:, None] == lax.iota(jnp.int32, slots)[None, :]).astype(jnp.bfloat16)
    rows = jnp.concatenate([x_rows, y_cot], axis=1)
    send = lax.dot_general(
        places, rows, (((0,), (0,)), ((), ())), preferred_element_type=jnp.float32
    ).astype(jnp.bfloat16)
    width = hidden_width + model_width
    recv, full = dispatch(send.reshape(PEERS, block_rows, width), weight_slice)
    recv = recv.reshape(slots, width)
    half = lax.broadcasted_iota(jnp.int32, (slots, 1), 0) % block_rows // capacity
    local_x, local_g = recv[:, :hidden_width], recv[:, hidden_width:]
    wide_x = jnp.concatenate(
        [jnp.where(half == h, local_x, jnp.zeros_like(local_x)) for h in range(2)], axis=1
    )
    outer = lax.dot_general(
        wide_x, local_g, (((0,), (0,)), ((), ())), preferred_element_type=jnp.float32
    )
    part = (outer * grad_factor).astype(jnp.bfloat16)
    part = part.reshape(2, GRID_Y, 2, slice_rows, model_width)
    weight_flat = full.reshape(2 * hidden_width, model_width)
    y_total = jnp.dot(wide_x, weight_flat, preferred_element_type=jnp.float32)
    dx_wide = lax.dot_general(
        local_g, weight_flat, (((1,), (1,)), ((), ())), preferred_element_type=jnp.float32
    )
    dx_total = jnp.where(half == 0, dx_wide[:, :hidden_width], dx_wide[:, hidden_width:])
    back = jnp.concatenate([dx_total, y_total], axis=1).astype(jnp.bfloat16)
    home, grad_pairs = give_back(back.reshape(PEERS, block_rows, width), part)
    home = home.reshape(slots, width)
    y_rows = jnp.dot(places, home[:, hidden_width:], preferred_element_type=jnp.float32).astype(
        jnp.bfloat16
    )
    x_grad = jnp.dot(places, home[:, :hidden_width], preferred_element_type=jnp.float32).astype(
        jnp.bfloat16
    )
    grad = jnp.sum(grad_pairs.astype(jnp.float32), axis=1)
    return (y_rows, x_grad) + adam_update(master_weight, grad, m_code, m_scale, v_code, v_scale)


def solution(mesh):
    state = P("grp", "rep", None)
    rows = P(("rep", "grp"), None)
    return jax.shard_map(
        per_device,
        mesh=mesh,
        in_specs=(state, state, state, state, state, P(), P(("rep", "grp")), rows, rows),
        out_specs=(rows, rows, state, state, state, state, state),
        check_vma=False,
    )
```

```python
import jax
import jax.numpy as jnp
from jax import lax
from jax.experimental import pallas as pl
from jax.experimental.pallas import tpu as pltpu
from jax.sharding import PartitionSpec as P

BLOCK = 128
ADAM_STEP = 100
GRID_X = 4
GRID_Y = 8
GRID_Z = 12
HALF_Z = GRID_Z // 2
PEERS = 2 * GRID_X * HALF_Z
MESH = pl.DeviceIdType.MESH
HOPS = 4
FIRST_ROWS = 4
FIRST_BACK = 24
VMEM_LIMIT = 40 * 1024 * 1024


beta_one = 0.9
beta_two = 0.95
learn_rate = 0.01


def adam_update(master_weight, grad, m_code, m_scale, v_code, v_scale):
    full_shape = master_weight.shape
    blocked = full_shape[:-1] + (full_shape[-1] // BLOCK, BLOCK)
    m_old = (m_code.astype(jnp.float32).reshape(blocked) * m_scale[..., None]).reshape(full_shape)
    v_old = (v_code.astype(jnp.float32).reshape(blocked) * v_scale[..., None]).reshape(full_shape)
    m_next = beta_one * m_old + (1.0 - beta_one) * grad
    v_next = beta_two * v_old + (1.0 - beta_two) * grad * grad
    corr_one = 1.0 - beta_one**ADAM_STEP
    corr_two = 1.0 - beta_two**ADAM_STEP
    step_size = m_next / corr_one / (jnp.sqrt(v_next / corr_two) + 1e-08)
    master_next = master_weight - learn_rate * step_size
    m_blocks = m_next.reshape(blocked)
    v_blocks = v_next.reshape(blocked)
    m_scale_next = jnp.max(jnp.abs(m_blocks), axis=-1) + 1e-06
    v_scale_next = jnp.max(v_blocks, axis=-1) + 1e-06
    m_code_next = (m_blocks / m_scale_next[..., None]).reshape(full_shape).astype(jnp.bfloat16)
    v_code_next = (v_blocks / v_scale_next[..., None]).reshape(full_shape).astype(jnp.bfloat16)
    return (master_next, m_code_next, m_scale_next, v_code_next, v_scale_next)


def offset_of(d, member):
    return jnp.where(d < 4 - member, d, d - HALF_Z)


class Place:
    def __init__(self):
        rep, grp = lax.axis_index("rep"), lax.axis_index("grp")
        self.y, self.c = rep // 2, rep % 2
        self.x, self.z = grp // GRID_Z, grp % GRID_Z

    def device(self, y=0, c=0, x=0, z=0):
        rep = (self.y + y + GRID_Y) % GRID_Y * 2 + (self.c + c) % 2
        grp = (self.x + x) % GRID_X * GRID_Z + (self.z + z + GRID_Z) % GRID_Z
        return rep, grp

    def slot(self, c, x, d):
        return ((self.c + c) % 2 * GRID_X + (self.x + x) % GRID_X) * HALF_Z + d


def signal(device):
    pl.semaphore_signal(
        pltpu.get_barrier_semaphore(), inc=1, device_id=device, device_id_type=MESH
    )


def peer(i):
    k, c, x = i // (2 * GRID_X), i // GRID_X % 2, i % GRID_X
    d = (3 + jnp.where(k % 2 == 1, (k + 1) // 2, -(k // 2))) % HALF_Z
    return c, x, d


def enter(place, sign):
    def greet(i, carry):
        c, x, d = peer(i)
        member = place.c if sign == 1 else (place.c + c) % 2

        @pl.when(jnp.logical_or(d != 0, i % (2 * GRID_X) != 0))
        def _():
            signal(place.device(c=c, x=x, z=-sign * offset_of(d, member)))

        return carry

    signal(place.device(z=HALF_Z // 2))
    signal(place.device(z=-(HALF_Z // 2)))
    signal(place.device(c=1, z=HALF_Z // 2))
    signal(place.device(y=1))
    signal(place.device(y=-1))
    lax.fori_loop(0, PEERS, greet, 0)
    pl.semaphore_wait(pltpu.get_barrier_semaphore(), PEERS - 1 + 5)


def rows_start(place, source, target, send_sem, recv_sem, sign, low, high):
    own = place.slot(0, 0, 0)
    if low == 0:
        pltpu.make_async_copy(source.at[own], target.at[own], recv_sem.at[own]).start()

    def step(i, carry):
        c, x, d = peer(i)
        member = (place.c + c) % 2 if sign == 1 else place.c
        there, here = place.slot(c, x, d), place.slot(0, 0, d)

        @pl.when(jnp.logical_or(d != 0, i % (2 * GRID_X) != 0))
        def _():
            remote(
                source.at[there], target.at[here], send_sem.at[there], recv_sem.at[here],
                place.device(c=c, x=x, z=sign * offset_of(d, member)),
            ).start()

        return carry

    lax.fori_loop(low, high, step, 0)


def rows_wait(place, source, target, send_sem, recv_sem, sign):
    own = place.slot(0, 0, 0)

    def step(i, carry):
        copy = pltpu.make_async_remote_copy(
            src_ref=source.at[i],
            dst_ref=target.at[i],
            send_sem=send_sem.at[i],
            recv_sem=recv_sem.at[i],
            device_id=place.device(y=1),
            device_id_type=MESH,
        )

        @pl.when(i != own)
        def _():
            copy.wait_send()
            copy.wait_recv()

        return carry

    lax.fori_loop(0, PEERS, step, 0)
    pltpu.make_async_copy(source.at[own], target.at[own], recv_sem.at[own]).wait()


def remote(source, target, send_sem, recv_sem, device):
    return pltpu.make_async_remote_copy(
        src_ref=source,
        dst_ref=target,
        send_sem=send_sem,
        recv_sem=recv_sem,
        device_id=device,
        device_id_type=MESH,
    )


def far_start(place, first, second, relay, send_sem, recv_sem):
    up = remote(
        first, relay.at[0], send_sem.at[0], recv_sem.at[0], place.device(z=HALF_Z // 2)
    )
    down = remote(
        second, relay.at[1], send_sem.at[1], recv_sem.at[1],
        place.device(c=1, z=-(HALF_Z // 2)),
    )
    up.start()
    down.start()
    return [up, down]


def far_relay(place, legs, relay, target_up, target_down, send_sem, recv_sem):
    up = remote(
        relay.at[0], target_up, send_sem.at[2], recv_sem.at[2], place.device(z=HALF_Z // 2)
    )
    down = remote(
        relay.at[1], target_down, send_sem.at[3], recv_sem.at[3],
        place.device(z=-(HALF_Z // 2)),
    )
    for leg, copy in zip(legs, (up, down)):
        leg.wait_recv()
        copy.start()
    return [up, down]


def ring_copy(place, source, target, send_sem, recv_sem, h, half, way, step):
    return remote(
        source, target, send_sem.at[h, half, way, step], recv_sem.at[h, half, way, step],
        place.device(y=1 - 2 * way),
    )


def dispatch_kernel(
    rows_ref, slice_ref, recv_ref, full_ref,
    relay, row_send, row_recv, far_send, far_recv, near_send, near_recv,
    ring_send, ring_recv, local_sem,
):
    place = Place()
    y, c = place.y, place.c
    enter(place, 1)
    own = pltpu.make_async_copy(slice_ref.at[c], full_ref.at[0, y, c], local_sem)
    own.start()
    near = remote(
        slice_ref.at[1 - c], full_ref.at[0, y, c], near_send, near_recv, place.device(c=1)
    )
    near.start()
    legs = far_start(place, slice_ref.at[c], slice_ref.at[1 - c], relay, far_send, far_recv)
    rows_start(place, rows_ref, recv_ref, row_send, row_recv, 1, 0, FIRST_ROWS)
    sent = []

    def ring(h, step):
        for half in range(2):
            for way in range(2):
                if step >= HOPS - (half != way):
                    continue
                if step > 0:
                    sent[index[h, half, way]].wait_recv()
                origin = (y - (1 - 2 * way) * step + GRID_Y) % GRID_Y
                block = full_ref.at[h, origin, half]
                copy = ring_copy(place, block, block, ring_send, ring_recv, h, half, way, step)
                copy.start()
                index[h, half, way] = len(sent)
                sent.append(copy)

    index = {}
    own.wait()
    near.wait()
    ring(0, 0)
    ring(0, 1)
    more = far_relay(
        place, legs, relay, full_ref.at[1, y, c], full_ref.at[1, y, 1 - c], far_send, far_recv
    )
    rows_start(place, rows_ref, recv_ref, row_send, row_recv, 1, FIRST_ROWS, PEERS)
    ring(0, 2)
    for copy in more:
        copy.wait_recv()
    ring(1, 0)
    ring(0, 3)
    ring(1, 1)
    ring(1, 2)
    ring(1, 3)
    for i in index.values():
        sent[i].wait_recv()
    for copy in legs + more + sent:
        copy.wait_send()
    rows_wait(place, rows_ref, recv_ref, row_send, row_recv, 1)


def return_kernel(
    rows_ref, part_ref, home_ref, grad_ref,
    relay, hold, total, row_send, row_recv, far_send, far_recv, near_send, near_recv,
    ring_send, ring_recv, local_sem,
):
    place = Place()
    y, c = place.y, place.c
    enter(place, -1)
    rows_start(place, rows_ref, home_ref, row_send, row_recv, -1, 0, FIRST_BACK)
    sent = []
    index = {}

    def ring(h, step):
        for half in range(2):
            for way in range(2):
                first = int(half != way)
                if step < first:
                    continue
                target = (y + (1 - 2 * way) * (HOPS - step) + GRID_Y) % GRID_Y
                if step == first:
                    source = part_ref.at[h, target, half]
                else:
                    sent[index[h, half, way]].wait_recv()
                    source = hold.at[h, way, step - 1, half]
                    source[...] = (
                        source[...].astype(jnp.float32)
                        + part_ref[h, target, half].astype(jnp.float32)
                    ).astype(jnp.bfloat16)
                copy = ring_copy(
                    place, source, hold.at[h, way, step, half],
                    ring_send, ring_recv, h, half, way, step,
                )
                copy.start()
                index[h, half, way] = len(sent)
                sent.append(copy)

    def finish(h):
        for half in range(2):
            for way in range(2):
                sent[index[h, half, way]].wait_recv()
        total[h] = (
            part_ref[h, y].astype(jnp.float32)
            + hold[h, 0, HOPS - 1].astype(jnp.float32)
            + hold[h, 1, HOPS - 1].astype(jnp.float32)
        ).astype(jnp.bfloat16)

    ring(1, 0)
    ring(1, 1)
    ring(1, 2)
    ring(0, 0)
    ring(1, 3)
    ring(0, 1)
    finish(1)
    legs = far_start(place, total.at[1, c], total.at[1, 1 - c], relay, far_send, far_recv)
    rows_start(place, rows_ref, home_ref, row_send, row_recv, -1, FIRST_BACK, PEERS)
    ring(0, 2)
    ring(0, 3)
    more = far_relay(
        place, legs, relay, grad_ref.at[c, 1], grad_ref.at[1 - c, 1], far_send, far_recv
    )
    finish(0)
    own = pltpu.make_async_copy(total.at[0, c], grad_ref.at[c, 0], local_sem)
    own.start()
    near = remote(
        total.at[0, 1 - c], grad_ref.at[c, 0], near_send, near_recv, place.device(c=1)
    )
    near.start()
    for copy in legs + sent:
        copy.wait_send()
    own.wait()
    near.wait()
    for copy in more:
        copy.wait()
    rows_wait(place, rows_ref, home_ref, row_send, row_recv, -1)


VMEM = pl.BlockSpec(memory_space=pltpu.VMEM)
DMA = pltpu.SemaphoreType.DMA


def dispatch(rows, weight_slice):
    members, slice_rows, width = weight_slice.shape
    return pl.pallas_call(
        dispatch_kernel,
        out_shape=(
            jax.ShapeDtypeStruct(rows.shape, rows.dtype),
            jax.ShapeDtypeStruct((2, GRID_Y, 2, slice_rows, width), weight_slice.dtype),
        ),
        in_specs=[VMEM] * 2,
        out_specs=(VMEM, VMEM),
        scratch_shapes=[
            pltpu.VMEM((2, slice_rows, width), weight_slice.dtype),
            DMA((PEERS,)), DMA((PEERS,)), DMA((4,)), DMA((4,)), DMA(()), DMA(()),
            DMA((2, 2, 2, HOPS)), DMA((2, 2, 2, HOPS)), DMA(()),
        ],
        compiler_params=pltpu.CompilerParams(
            collective_id=0, has_side_effects=True, vmem_limit_bytes=VMEM_LIMIT
        ),
        name="dispatch",
    )(rows, weight_slice)


def give_back(rows, part):
    slice_rows, width = part.shape[-2:]
    return pl.pallas_call(
        return_kernel,
        out_shape=(
            jax.ShapeDtypeStruct(rows.shape, rows.dtype),
            jax.ShapeDtypeStruct((2, 2, slice_rows, width), part.dtype),
        ),
        in_specs=[VMEM] * 2,
        out_specs=(VMEM, VMEM),
        scratch_shapes=[
            pltpu.VMEM((2, slice_rows, width), part.dtype),
            pltpu.VMEM((2, 2, HOPS, 2, slice_rows, width), part.dtype),
            pltpu.VMEM((2, 2, slice_rows, width), part.dtype),
            DMA((PEERS,)), DMA((PEERS,)), DMA((4,)), DMA((4,)), DMA(()), DMA(()),
            DMA((2, 2, 2, HOPS)), DMA((2, 2, 2, HOPS)), DMA(()),
        ],
        compiler_params=pltpu.CompilerParams(
            collective_id=1, has_side_effects=True, vmem_limit_bytes=VMEM_LIMIT
        ),
        name="give_back",
    )(rows, part)


def per_device(master_weight, m_code, m_scale, v_code, v_scale, placement, route, x_rows, y_cot):
    members, slice_rows, model_width = master_weight.shape
    row_count, hidden_width = x_rows.shape
    expert_count = placement.shape[0]
    groups = lax.axis_size("grp")
    replicas = lax.axis_size("rep")
    grad_factor = float(row_count * groups * replicas // expert_count) ** (-0.5)
    capacity = max(2, (3 * row_count + 2 * expert_count - 1) // (2 * expert_count))
    block_rows = 2 * capacity
    slots = PEERS * block_rows
    weight_slice = master_weight.astype(jnp.bfloat16)
    expert_ids = lax.iota(jnp.int32, expert_count)
    route_hot = (route[:, None] == expert_ids[None, :]).astype(jnp.int32)
    position = jnp.sum(route_hot * (jnp.cumsum(route_hot, axis=0) - 1), axis=1)
    slot = jnp.sum(jnp.where(placement[None, :] == route[:, None], expert_ids[None, :], 0), axis=1)
    here_z = lax.axis_index("grp") % GRID_Z
    core, chip_x, chip_z = slot % members, slot // members // GRID_Z, slot // members % GRID_Z
    d = (chip_z - here_z + GRID_Z) % HALF_Z
    far = ((here_z + offset_of(d, core) + GRID_Z) % GRID_Z != chip_z).astype(jnp.int32)
    target = ((core * GRID_X + chip_x) * HALF_Z + d) * block_rows + far * capacity + position
    places = (target[:, None] == lax.iota(jnp.int32, slots)[None, :]).astype(jnp.bfloat16)
    rows = jnp.concatenate([x_rows, y_cot], axis=1)
    send = lax.dot_general(
        places, rows, (((0,), (0,)), ((), ())), preferred_element_type=jnp.float32
    ).astype(jnp.bfloat16)
    width = hidden_width + model_width
    recv, full = dispatch(send.reshape(PEERS, block_rows, width), weight_slice)
    recv = recv.reshape(slots, width)
    half = lax.broadcasted_iota(jnp.int32, (slots, 1), 0) % block_rows // capacity
    local_x, local_g = recv[:, :hidden_width], recv[:, hidden_width:]
    wide_x = jnp.concatenate(
        [jnp.where(half == h, local_x, jnp.zeros_like(local_x)) for h in range(2)], axis=1
    )
    outer = lax.dot_general(
        wide_x, local_g, (((0,), (0,)), ((), ())), preferred_element_type=jnp.float32
    )
    part = (outer * grad_factor).astype(jnp.bfloat16)
    part = part.reshape(2, GRID_Y, 2, slice_rows, model_width)
    weight_flat = full.reshape(2 * hidden_width, model_width)
    y_total = jnp.dot(wide_x, weight_flat, preferred_element_type=jnp.float32)
    dx_wide = lax.dot_general(
        local_g, weight_flat, (((1,), (1,)), ((), ())), preferred_element_type=jnp.float32
    )
    dx_total = jnp.where(half == 0, dx_wide[:, :hidden_width], dx_wide[:, hidden_width:])
    back = jnp.concatenate([dx_total, y_total], axis=1).astype(jnp.bfloat16)
    home, grad_pairs = give_back(back.reshape(PEERS, block_rows, width), part)
    home = home.reshape(slots, width)
    y_rows = jnp.dot(places, home[:, hidden_width:], preferred_element_type=jnp.float32).astype(
        jnp.bfloat16
    )
    x_grad = jnp.dot(places, home[:, :hidden_width], preferred_element_type=jnp.float32).astype(
        jnp.bfloat16
    )
    grad = jnp.sum(grad_pairs.astype(jnp.float32), axis=1)
    return (y_rows, x_grad) + adam_update(master_weight, grad, m_code, m_scale, v_code, v_scale)


def solution(mesh):
    state = P("grp", "rep", None)
    rows = P(("rep", "grp"), None)
    return jax.shard_map(
        per_device,
        mesh=mesh,
        in_specs=(state, state, state, state, state, P(), P(("rep", "grp")), rows, rows),
        out_specs=(rows, rows, state, state, state, state, state),
        check_vma=False,
    )
```

```python
import jax
import jax.numpy as jnp
from jax import lax
from jax.experimental import pallas as pl
from jax.experimental.pallas import tpu as pltpu
from jax.sharding import PartitionSpec as P

BLOCK = 128
ADAM_STEP = 100
GRID_X = 4
GRID_Y = 8
GRID_Z = 12
HALF_Z = GRID_Z // 2
PEERS = 2 * GRID_X * HALF_Z
MESH = pl.DeviceIdType.MESH
HOPS = 4
FIRST_ROWS = 4
FIRST_BACK = 24
VMEM_LIMIT = 40 * 1024 * 1024
FIRST_LIMIT = VMEM_LIMIT


beta_one = 0.9
beta_two = 0.95
learn_rate = 0.01


def adam_kernel(
    weight_ref, m_code_ref, m_scale_ref, v_code_ref, v_scale_ref, grad_ref,
    weight_out, m_code_out, m_scale_out, v_code_out, v_scale_out,
):
    members, rows, width = weight_ref.shape
    i = lax.broadcasted_iota(jnp.int32, (rows, rows), 0)
    j = lax.broadcasted_iota(jnp.int32, (rows, rows), 1)
    corr_one = 1.0 - beta_one**ADAM_STEP
    corr_two = 1.0 - beta_two**ADAM_STEP

    def load_scale(ref, e, b):
        return jnp.sum(jnp.where(i == j, ref[e, b : b + 1, :], 0.0), axis=1, keepdims=True)

    def store_scale(ref, e, b, value):
        ref[e, b : b + 1, :] = jnp.sum(jnp.where(i == j, value, 0.0), axis=0, keepdims=True)

    for e in range(members):
        for b in range(width // BLOCK):
            at = slice(b * BLOCK, (b + 1) * BLOCK)
            grad = grad_ref[e, 0, :, at].astype(jnp.float32) + grad_ref[e, 1, :, at].astype(
                jnp.float32
            )
            m_old = m_code_ref[e, :, at].astype(jnp.float32) * load_scale(m_scale_ref, e, b)
            v_old = v_code_ref[e, :, at].astype(jnp.float32) * load_scale(v_scale_ref, e, b)
            m_next = beta_one * m_old + (1.0 - beta_one) * grad
            v_next = beta_two * v_old + (1.0 - beta_two) * grad * grad
            step_size = m_next / corr_one / (jnp.sqrt(v_next / corr_two) + 1e-08)
            weight_out[e, :, at] = weight_ref[e, :, at] - learn_rate * step_size
            m_scale_next = jnp.max(jnp.abs(m_next), axis=-1, keepdims=True) + 1e-06
            v_scale_next = jnp.max(v_next, axis=-1, keepdims=True) + 1e-06
            m_code_out[e, :, at] = (m_next / m_scale_next).astype(jnp.bfloat16)
            v_code_out[e, :, at] = (v_next / v_scale_next).astype(jnp.bfloat16)
            store_scale(m_scale_out, e, b, m_scale_next)
            store_scale(v_scale_out, e, b, v_scale_next)


def adam_update(master_weight, grad_pairs, m_code, m_scale, v_code, v_scale):
    turned = [jnp.swapaxes(scale, 1, 2) for scale in (m_scale, v_scale)]
    like = [
        jax.ShapeDtypeStruct(array.shape, array.dtype)
        for array in (master_weight, m_code, turned[0], v_code, turned[1])
    ]
    weight, m_next, m_rows, v_next, v_rows = pl.pallas_call(
        adam_kernel,
        out_shape=like,
        in_specs=[pl.BlockSpec(memory_space=pltpu.VMEM)] * 6,
        out_specs=[pl.BlockSpec(memory_space=pltpu.VMEM)] * 5,
        compiler_params=pltpu.CompilerParams(vmem_limit_bytes=VMEM_LIMIT // 2),
        name="adam",
    )(master_weight, m_code, turned[0], v_code, turned[1], grad_pairs)
    return (weight, m_next, jnp.swapaxes(m_rows, 1, 2), v_next, jnp.swapaxes(v_rows, 1, 2))


def offset_of(d, member):
    return jnp.where(d < 4 - member, d, d - HALF_Z)


class Place:
    def __init__(self):
        rep, grp = lax.axis_index("rep"), lax.axis_index("grp")
        self.y, self.c = rep // 2, rep % 2
        self.x, self.z = grp // GRID_Z, grp % GRID_Z

    def device(self, y=0, c=0, x=0, z=0):
        rep = (self.y + y + GRID_Y) % GRID_Y * 2 + (self.c + c) % 2
        grp = (self.x + x) % GRID_X * GRID_Z + (self.z + z + GRID_Z) % GRID_Z
        return rep, grp

    def slot(self, c, x, d):
        return ((self.c + c) % 2 * GRID_X + (self.x + x) % GRID_X) * HALF_Z + d


def signal(device):
    pl.semaphore_signal(
        pltpu.get_barrier_semaphore(), inc=1, device_id=device, device_id_type=MESH
    )


def peer(i):
    k, c, x = i // (2 * GRID_X), i // GRID_X % 2, i % GRID_X
    d = (3 + jnp.where(k % 2 == 1, (k + 1) // 2, -(k // 2))) % HALF_Z
    return c, x, d


def greet_all(place, sign):
    def greet(i, carry):
        c, x, d = peer(i)
        member = place.c if sign == 1 else (place.c + c) % 2

        @pl.when(jnp.logical_or(d != 0, i % (2 * GRID_X) != 0))
        def _():
            signal(place.device(c=c, x=x, z=-sign * offset_of(d, member)))

        return carry

    signal(place.device(z=HALF_Z // 2))
    signal(place.device(z=-(HALF_Z // 2)))
    signal(place.device(c=1, z=HALF_Z // 2))
    signal(place.device(y=1))
    signal(place.device(y=-1))
    lax.fori_loop(0, PEERS, greet, 0)


def wait_all():
    pl.semaphore_wait(pltpu.get_barrier_semaphore(), PEERS - 1 + 5)


def column(row):
    size = row.shape[1]
    i = lax.broadcasted_iota(jnp.int32, (size, size), 0)
    j = lax.broadcasted_iota(jnp.int32, (size, size), 1)
    return jnp.sum(jnp.where(i == j, row, 0.0), axis=1, keepdims=True)


def targets(place, placement, route):
    experts, rows = placement.shape[1], route.shape[1]
    route = route.astype(jnp.float32)
    i = lax.broadcasted_iota(jnp.int32, (rows, rows), 0)
    j = lax.broadcasted_iota(jnp.int32, (rows, rows), 1)
    earlier = jnp.logical_and(column(route) == route, i < j)
    position = jnp.sum(jnp.where(earlier, 1.0, 0.0), axis=0, keepdims=True).astype(jnp.int32)
    ids = lax.broadcasted_iota(jnp.int32, (experts, rows), 0).astype(jnp.float32)
    hit = column(placement.astype(jnp.float32)) == route
    slot = jnp.sum(jnp.where(hit, ids, 0.0), axis=0, keepdims=True).astype(jnp.int32)

    def count(value, step, most):
        return sum(jnp.where(value >= k * step, 1, 0) for k in range(1, most))

    core, group = slot & 1, slot >> 1
    chip_x = count(group, GRID_Z, GRID_X)
    chip_z = group - GRID_Z * chip_x
    ahead = chip_z - place.z + GRID_Z
    d = ahead - HALF_Z * count(ahead, HALF_Z, 4)
    delta = place.z + offset_of(d, core) - chip_z
    near = jnp.logical_or(delta == 0, jnp.logical_or(delta == GRID_Z, delta == -GRID_Z))
    far = jnp.where(near, 0, 1)
    return ((core * GRID_X + chip_x) * HALF_Z + d) * 8 + far * 4 + position


def rows_start(place, source, target, send_sem, recv_sem, sign, low, high):
    own = place.slot(0, 0, 0)
    if low == 0:
        pltpu.make_async_copy(source.at[own], target.at[own], recv_sem.at[own]).start()

    def step(i, carry):
        c, x, d = peer(i)
        member = (place.c + c) % 2 if sign == 1 else place.c
        there, here = place.slot(c, x, d), place.slot(0, 0, d)

        @pl.when(jnp.logical_or(d != 0, i % (2 * GRID_X) != 0))
        def _():
            remote(
                source.at[there], target.at[here], send_sem.at[there], recv_sem.at[here],
                place.device(c=c, x=x, z=sign * offset_of(d, member)),
            ).start()

        return carry

    lax.fori_loop(low, high, step, 0)


def rows_wait(place, source, target, send_sem, recv_sem, sign):
    own = place.slot(0, 0, 0)

    def step(i, carry):
        copy = pltpu.make_async_remote_copy(
            src_ref=source.at[i],
            dst_ref=target.at[i],
            send_sem=send_sem.at[i],
            recv_sem=recv_sem.at[i],
            device_id=place.device(y=1),
            device_id_type=MESH,
        )

        @pl.when(i != own)
        def _():
            copy.wait_send()
            copy.wait_recv()

        return carry

    lax.fori_loop(0, PEERS, step, 0)
    pltpu.make_async_copy(source.at[own], target.at[own], recv_sem.at[own]).wait()


def remote(source, target, send_sem, recv_sem, device):
    return pltpu.make_async_remote_copy(
        src_ref=source,
        dst_ref=target,
        send_sem=send_sem,
        recv_sem=recv_sem,
        device_id=device,
        device_id_type=MESH,
    )


def far_start(place, first, second, relay, send_sem, recv_sem):
    up = remote(
        first, relay.at[0], send_sem.at[0], recv_sem.at[0], place.device(z=HALF_Z // 2)
    )
    down = remote(
        second, relay.at[1], send_sem.at[1], recv_sem.at[1],
        place.device(c=1, z=-(HALF_Z // 2)),
    )
    up.start()
    down.start()
    return [up, down]


def far_relay(place, legs, relay, target_up, target_down, send_sem, recv_sem):
    up = remote(
        relay.at[0], target_up, send_sem.at[2], recv_sem.at[2], place.device(z=HALF_Z // 2)
    )
    down = remote(
        relay.at[1], target_down, send_sem.at[3], recv_sem.at[3],
        place.device(z=-(HALF_Z // 2)),
    )
    for leg, copy in zip(legs, (up, down)):
        leg.wait_recv()
        copy.start()
    return [up, down]


def ring_copy(place, source, target, send_sem, recv_sem, h, half, way, step):
    return remote(
        source, target, send_sem.at[h, half, way, step], recv_sem.at[h, half, way, step],
        place.device(y=1 - 2 * way),
    )


def dispatch_kernel(
    placement_ref, route_ref, x_hbm, g_hbm, weight_hbm, recv_ref, full_ref, target_ref,
    x_ref, g_ref, weight_ref, rows_ref, slice_ref, load_sem, relay, row_send, row_recv, far_send, far_recv, near_send, near_recv,
    ring_send, ring_recv, local_sem,
):
    place = Place()
    y, c = place.y, place.c
    loads = [
        pltpu.make_async_copy(source, into, load_sem.at[i])
        for i, (source, into) in enumerate(
            ((weight_hbm, weight_ref), (x_hbm, x_ref), (g_hbm, g_ref))
        )
    ]
    for load in loads:
        load.start()
    greet_all(place, 1)
    target = targets(place, placement_ref[...], route_ref[...])
    target_ref[...] = target
    slots, row_count = PEERS * 8, x_ref.shape[0]
    places = lax.broadcasted_iota(jnp.int32, (slots, row_count), 0) == target
    places = jnp.where(places, 1.0, 0.0).astype(jnp.bfloat16)
    loads[0].wait()
    slice_ref[...] = weight_ref[...].astype(jnp.bfloat16)
    loads[1].wait()
    hidden = x_ref.shape[1]
    rows_ref[:, :, :hidden] = (
        jnp.dot(places, x_ref[...], preferred_element_type=jnp.float32)
        .reshape(PEERS, 8, hidden)
        .astype(jnp.bfloat16)
    )
    loads[2].wait()
    for j in range(0, g_ref.shape[1], 512):
        rows_ref[:, :, hidden + j : hidden + j + 512] = (
            jnp.dot(places, g_ref[:, j : j + 512], preferred_element_type=jnp.float32)
            .reshape(PEERS, 8, 512)
            .astype(jnp.bfloat16)
        )
    wait_all()
    own = pltpu.make_async_copy(slice_ref.at[c], full_ref.at[0, y, c], local_sem)
    own.start()
    near = remote(
        slice_ref.at[1 - c], full_ref.at[0, y, c], near_send, near_recv, place.device(c=1)
    )
    near.start()
    legs = far_start(place, slice_ref.at[c], slice_ref.at[1 - c], relay, far_send, far_recv)
    rows_start(place, rows_ref, recv_ref, row_send, row_recv, 1, 0, FIRST_ROWS)
    sent = []

    def ring(h, step):
        for half in range(2):
            for way in range(2):
                if step >= HOPS - (half != way):
                    continue
                if step > 0:
                    sent[index[h, half, way]].wait_recv()
                origin = (y - (1 - 2 * way) * step + GRID_Y) % GRID_Y
                block = full_ref.at[h, origin, half]
                copy = ring_copy(place, block, block, ring_send, ring_recv, h, half, way, step)
                copy.start()
                index[h, half, way] = len(sent)
                sent.append(copy)

    index = {}
    own.wait()
    near.wait()
    ring(0, 0)
    ring(0, 1)
    more = far_relay(
        place, legs, relay, full_ref.at[1, y, c], full_ref.at[1, y, 1 - c], far_send, far_recv
    )
    rows_start(place, rows_ref, recv_ref, row_send, row_recv, 1, FIRST_ROWS, PEERS)
    ring(0, 2)
    for copy in more:
        copy.wait_recv()
    ring(1, 0)
    ring(0, 3)
    ring(1, 1)
    ring(1, 2)
    ring(1, 3)
    for i in index.values():
        sent[i].wait_recv()
    for copy in legs + more + sent:
        copy.wait_send()
    rows_wait(place, rows_ref, recv_ref, row_send, row_recv, 1)


def return_kernel(
    rows_ref, part_ref, home_ref, grad_ref,
    relay, hold, total, row_send, row_recv, far_send, far_recv, near_send, near_recv,
    ring_send, ring_recv, local_sem,
):
    place = Place()
    y, c = place.y, place.c
    greet_all(place, -1)
    wait_all()
    rows_start(place, rows_ref, home_ref, row_send, row_recv, -1, 0, FIRST_BACK)
    sent = []
    index = {}

    def ring(h, step):
        for half in range(2):
            for way in range(2):
                first = int(half != way)
                if step < first:
                    continue
                target = (y + (1 - 2 * way) * (HOPS - step) + GRID_Y) % GRID_Y
                if step == first:
                    source = part_ref.at[h, target, half]
                else:
                    sent[index[h, half, way]].wait_recv()
                    source = hold.at[h, way, step - 1, half]
                    source[...] = (
                        source[...].astype(jnp.float32)
                        + part_ref[h, target, half].astype(jnp.float32)
                    ).astype(jnp.bfloat16)
                copy = ring_copy(
                    place, source, hold.at[h, way, step, half],
                    ring_send, ring_recv, h, half, way, step,
                )
                copy.start()
                index[h, half, way] = len(sent)
                sent.append(copy)

    def finish(h):
        for half in range(2):
            for way in range(2):
                sent[index[h, half, way]].wait_recv()
        total[h] = (
            part_ref[h, y].astype(jnp.float32)
            + hold[h, 0, HOPS - 1].astype(jnp.float32)
            + hold[h, 1, HOPS - 1].astype(jnp.float32)
        ).astype(jnp.bfloat16)

    ring(1, 0)
    ring(1, 1)
    ring(1, 2)
    ring(0, 0)
    ring(1, 3)
    ring(0, 1)
    finish(1)
    legs = far_start(place, total.at[1, c], total.at[1, 1 - c], relay, far_send, far_recv)
    rows_start(place, rows_ref, home_ref, row_send, row_recv, -1, FIRST_BACK, PEERS)
    ring(0, 2)
    ring(0, 3)
    more = far_relay(
        place, legs, relay, grad_ref.at[c, 1], grad_ref.at[1 - c, 1], far_send, far_recv
    )
    finish(0)
    own = pltpu.make_async_copy(total.at[0, c], grad_ref.at[c, 0], local_sem)
    own.start()
    near = remote(
        total.at[0, 1 - c], grad_ref.at[c, 0], near_send, near_recv, place.device(c=1)
    )
    near.start()
    for copy in legs + sent:
        copy.wait_send()
    own.wait()
    near.wait()
    for copy in more:
        copy.wait()
    rows_wait(place, rows_ref, home_ref, row_send, row_recv, -1)


VMEM = pl.BlockSpec(memory_space=pltpu.VMEM)
DMA = pltpu.SemaphoreType.DMA


def dispatch(placement, route, x_rows, y_cot, master_weight):
    members, slice_rows, width = master_weight.shape
    row_count, hidden = x_rows.shape
    hbm = pl.BlockSpec(memory_space=pltpu.HBM)
    low = jnp.bfloat16
    return pl.pallas_call(
        dispatch_kernel,
        out_shape=(
            jax.ShapeDtypeStruct((PEERS, 8, hidden + width), low),
            jax.ShapeDtypeStruct((2, GRID_Y, 2, slice_rows, width), low),
            jax.ShapeDtypeStruct((1, row_count), jnp.int32),
        ),
        in_specs=[VMEM, VMEM, hbm, hbm, hbm],
        out_specs=(VMEM, VMEM, VMEM),
        scratch_shapes=[
            pltpu.VMEM(x_rows.shape, low),
            pltpu.VMEM(y_cot.shape, low),
            pltpu.VMEM(master_weight.shape, jnp.float32),
            pltpu.VMEM((PEERS, 8, hidden + width), low),
            pltpu.VMEM(master_weight.shape, low),
            DMA((3,)),
            pltpu.VMEM((2, slice_rows, width), low),
            DMA((PEERS,)), DMA((PEERS,)), DMA((4,)), DMA((4,)), DMA(()), DMA(()),
            DMA((2, 2, 2, HOPS)), DMA((2, 2, 2, HOPS)), DMA(()),
        ],
        compiler_params=pltpu.CompilerParams(
            collective_id=0, has_side_effects=True, vmem_limit_bytes=FIRST_LIMIT
        ),
        name="dispatch",
    )(
        *(
            pltpu.with_memory_space_constraint(array, pltpu.HBM)
            for array in (
                placement.reshape(1, -1), route.reshape(1, -1), x_rows, y_cot, master_weight
            )
        )
    )


def give_back(rows, part):
    slice_rows, width = part.shape[-2:]
    return pl.pallas_call(
        return_kernel,
        out_shape=(
            jax.ShapeDtypeStruct(rows.shape, rows.dtype),
            jax.ShapeDtypeStruct((2, 2, slice_rows, width), part.dtype),
        ),
        in_specs=[VMEM] * 2,
        out_specs=(VMEM, VMEM),
        scratch_shapes=[
            pltpu.VMEM((2, slice_rows, width), part.dtype),
            pltpu.VMEM((2, 2, HOPS, 2, slice_rows, width), part.dtype),
            pltpu.VMEM((2, 2, slice_rows, width), part.dtype),
            DMA((PEERS,)), DMA((PEERS,)), DMA((4,)), DMA((4,)), DMA(()), DMA(()),
            DMA((2, 2, 2, HOPS)), DMA((2, 2, 2, HOPS)), DMA(()),
        ],
        compiler_params=pltpu.CompilerParams(
            collective_id=1, has_side_effects=True, vmem_limit_bytes=VMEM_LIMIT
        ),
        name="give_back",
    )(rows, part)


def per_device(master_weight, m_code, m_scale, v_code, v_scale, placement, route, x_rows, y_cot):
    members, slice_rows, model_width = master_weight.shape
    row_count, hidden_width = x_rows.shape
    expert_count = placement.shape[0]
    groups = lax.axis_size("grp")
    replicas = lax.axis_size("rep")
    grad_factor = float(row_count * groups * replicas // expert_count) ** (-0.5)
    capacity = max(2, (3 * row_count + 2 * expert_count - 1) // (2 * expert_count))
    block_rows = 2 * capacity
    slots = PEERS * block_rows
    width = hidden_width + model_width
    recv, full, target = dispatch(placement, route, x_rows, y_cot, master_weight)
    places = (target.reshape(-1, 1) == lax.iota(jnp.int32, slots)[None, :]).astype(jnp.bfloat16)
    recv = recv.reshape(slots, width)
    half = lax.broadcasted_iota(jnp.int32, (slots, 1), 0) % block_rows // capacity
    local_x, local_g = recv[:, :hidden_width], recv[:, hidden_width:]
    wide_x = jnp.concatenate(
        [jnp.where(half == h, local_x, jnp.zeros_like(local_x)) for h in range(2)], axis=1
    )
    outer = lax.dot_general(
        wide_x, local_g, (((0,), (0,)), ((), ())), preferred_element_type=jnp.float32
    )
    part = (outer * grad_factor).astype(jnp.bfloat16)
    part = part.reshape(2, GRID_Y, 2, slice_rows, model_width)
    weight_flat = full.reshape(2 * hidden_width, model_width)
    y_total = jnp.dot(wide_x, weight_flat, preferred_element_type=jnp.float32)
    dx_wide = lax.dot_general(
        local_g, weight_flat, (((1,), (1,)), ((), ())), preferred_element_type=jnp.float32
    )
    dx_total = jnp.where(half == 0, dx_wide[:, :hidden_width], dx_wide[:, hidden_width:])
    back = jnp.concatenate([dx_total, y_total], axis=1).astype(jnp.bfloat16)
    home, grad_pairs = give_back(back.reshape(PEERS, block_rows, width), part)
    home = home.reshape(slots, width)
    y_rows = jnp.dot(places, home[:, hidden_width:], preferred_element_type=jnp.float32).astype(
        jnp.bfloat16
    )
    x_grad = jnp.dot(places, home[:, :hidden_width], preferred_element_type=jnp.float32).astype(
        jnp.bfloat16
    )
    return (y_rows, x_grad) + adam_update(master_weight, grad_pairs, m_code, m_scale, v_code, v_scale)


def solution(mesh):
    state = P("grp", "rep", None)
    rows = P(("rep", "grp"), None)
    return jax.shard_map(
        per_device,
        mesh=mesh,
        in_specs=(state, state, state, state, state, P(), P(("rep", "grp")), rows, rows),
        out_specs=(rows, rows, state, state, state, state, state),
        check_vma=False,
    )
```

```python
import jax
import jax.numpy as jnp
from jax import lax
from jax.experimental import pallas as pl
from jax.experimental.pallas import tpu as pltpu
from jax.sharding import PartitionSpec as P

BLOCK = 128
ADAM_STEP = 100
GRID_X = 4
GRID_Y = 8
GRID_Z = 12
HALF_Z = GRID_Z // 2
PEERS = 2 * GRID_X * HALF_Z
MESH = pl.DeviceIdType.MESH
HOPS = 4
FIRST_ROWS = 2
FIRST_BACK = 24
VMEM_LIMIT = 40 * 1024 * 1024
FIRST_LIMIT = VMEM_LIMIT


beta_one = 0.9
beta_two = 0.95
learn_rate = 0.01


def adam_kernel(
    weight_ref, m_code_ref, m_scale_ref, v_code_ref, v_scale_ref, grad_ref,
    weight_out, m_code_out, m_scale_out, v_code_out, v_scale_out,
):
    members, rows, width = weight_ref.shape
    i = lax.broadcasted_iota(jnp.int32, (rows, rows), 0)
    j = lax.broadcasted_iota(jnp.int32, (rows, rows), 1)
    corr_one = 1.0 - beta_one**ADAM_STEP
    corr_two = 1.0 - beta_two**ADAM_STEP

    def load_scale(ref, e, b):
        return jnp.sum(jnp.where(i == j, ref[e, b : b + 1, :], 0.0), axis=1, keepdims=True)

    def store_scale(ref, e, b, value):
        ref[e, b : b + 1, :] = jnp.sum(jnp.where(i == j, value, 0.0), axis=0, keepdims=True)

    for e in range(members):
        for b in range(width // BLOCK):
            at = slice(b * BLOCK, (b + 1) * BLOCK)
            grad = grad_ref[e, 0, :, at].astype(jnp.float32) + grad_ref[e, 1, :, at].astype(
                jnp.float32
            )
            m_old = m_code_ref[e, :, at].astype(jnp.float32) * load_scale(m_scale_ref, e, b)
            v_old = v_code_ref[e, :, at].astype(jnp.float32) * load_scale(v_scale_ref, e, b)
            m_next = beta_one * m_old + (1.0 - beta_one) * grad
            v_next = beta_two * v_old + (1.0 - beta_two) * grad * grad
            step_size = m_next / corr_one / (jnp.sqrt(v_next / corr_two) + 1e-08)
            weight_out[e, :, at] = weight_ref[e, :, at] - learn_rate * step_size
            m_scale_next = jnp.max(jnp.abs(m_next), axis=-1, keepdims=True) + 1e-06
            v_scale_next = jnp.max(v_next, axis=-1, keepdims=True) + 1e-06
            m_code_out[e, :, at] = (m_next / m_scale_next).astype(jnp.bfloat16)
            v_code_out[e, :, at] = (v_next / v_scale_next).astype(jnp.bfloat16)
            store_scale(m_scale_out, e, b, m_scale_next)
            store_scale(v_scale_out, e, b, v_scale_next)


def adam_update(master_weight, grad_pairs, m_code, m_scale, v_code, v_scale):
    turned = [jnp.swapaxes(scale, 1, 2) for scale in (m_scale, v_scale)]
    like = [
        jax.ShapeDtypeStruct(array.shape, array.dtype)
        for array in (master_weight, m_code, turned[0], v_code, turned[1])
    ]
    weight, m_next, m_rows, v_next, v_rows = pl.pallas_call(
        adam_kernel,
        out_shape=like,
        in_specs=[pl.BlockSpec(memory_space=pltpu.VMEM)] * 6,
        out_specs=[pl.BlockSpec(memory_space=pltpu.VMEM)] * 5,
        compiler_params=pltpu.CompilerParams(vmem_limit_bytes=VMEM_LIMIT // 2),
        name="adam",
    )(master_weight, m_code, turned[0], v_code, turned[1], grad_pairs)
    return (weight, m_next, jnp.swapaxes(m_rows, 1, 2), v_next, jnp.swapaxes(v_rows, 1, 2))


def offset_of(d, member):
    return jnp.where(d < 4 - member, d, d - HALF_Z)


class Place:
    def __init__(self):
        rep, grp = lax.axis_index("rep"), lax.axis_index("grp")
        self.y, self.c = rep // 2, rep % 2
        self.x, self.z = grp // GRID_Z, grp % GRID_Z

    def device(self, y=0, c=0, x=0, z=0):
        rep = (self.y + y + GRID_Y) % GRID_Y * 2 + (self.c + c) % 2
        grp = (self.x + x) % GRID_X * GRID_Z + (self.z + z + GRID_Z) % GRID_Z
        return rep, grp

    def slot(self, c, x, d):
        return ((self.c + c) % 2 * GRID_X + (self.x + x) % GRID_X) * HALF_Z + d


def signal(device):
    pl.semaphore_signal(
        pltpu.get_barrier_semaphore(), inc=1, device_id=device, device_id_type=MESH
    )


def peer(i):
    k, c, x = i // (2 * GRID_X), i // GRID_X % 2, i % GRID_X
    d = (3 + jnp.where(k % 2 == 1, (k + 1) // 2, -(k // 2))) % HALF_Z
    return c, x, d


def greet_all(place, sign):
    def greet(i, carry):
        c, x, d = peer(i)
        member = place.c if sign == 1 else (place.c + c) % 2

        @pl.when(jnp.logical_or(d != 0, i % (2 * GRID_X) != 0))
        def _():
            signal(place.device(c=c, x=x, z=-sign * offset_of(d, member)))

        return carry

    signal(place.device(z=HALF_Z // 2))
    signal(place.device(z=-(HALF_Z // 2)))
    signal(place.device(c=1, z=HALF_Z // 2))
    signal(place.device(y=1))
    signal(place.device(y=-1))
    lax.fori_loop(0, PEERS, greet, 0)


def wait_all():
    pl.semaphore_wait(pltpu.get_barrier_semaphore(), PEERS - 1 + 5)


def column(row):
    size = row.shape[1]
    i = lax.broadcasted_iota(jnp.int32, (size, size), 0)
    j = lax.broadcasted_iota(jnp.int32, (size, size), 1)
    return jnp.sum(jnp.where(i == j, row, 0.0), axis=1, keepdims=True)


def targets(place, placement, route):
    experts, rows = placement.shape[1], route.shape[1]
    route = route.astype(jnp.float32)
    i = lax.broadcasted_iota(jnp.int32, (rows, rows), 0)
    j = lax.broadcasted_iota(jnp.int32, (rows, rows), 1)
    earlier = jnp.logical_and(column(route) == route, i < j)
    position = jnp.sum(jnp.where(earlier, 1.0, 0.0), axis=0, keepdims=True).astype(jnp.int32)
    ids = lax.broadcasted_iota(jnp.int32, (experts, rows), 0).astype(jnp.float32)
    hit = column(placement.astype(jnp.float32)) == route
    slot = jnp.sum(jnp.where(hit, ids, 0.0), axis=0, keepdims=True).astype(jnp.int32)

    def count(value, step, most):
        return sum(jnp.where(value >= k * step, 1, 0) for k in range(1, most))

    core, group = slot & 1, slot >> 1
    chip_x = count(group, GRID_Z, GRID_X)
    chip_z = group - GRID_Z * chip_x
    ahead = chip_z - place.z + GRID_Z
    d = ahead - HALF_Z * count(ahead, HALF_Z, 4)
    delta = place.z + offset_of(d, core) - chip_z
    near = jnp.logical_or(delta == 0, jnp.logical_or(delta == GRID_Z, delta == -GRID_Z))
    far = jnp.where(near, 0, 1)
    return ((core * GRID_X + chip_x) * HALF_Z + d) * 8 + far * 4 + position


def rows_start(place, source, target, send_sem, recv_sem, sign, low, high):
    own = place.slot(0, 0, 0)
    if low == 0:
        pltpu.make_async_copy(source.at[own], target.at[own], recv_sem.at[own]).start()

    def step(i, carry):
        c, x, d = peer(i)
        member = (place.c + c) % 2 if sign == 1 else place.c
        there, here = place.slot(c, x, d), place.slot(0, 0, d)

        @pl.when(jnp.logical_or(d != 0, i % (2 * GRID_X) != 0))
        def _():
            remote(
                source.at[there], target.at[here], send_sem.at[there], recv_sem.at[here],
                place.device(c=c, x=x, z=sign * offset_of(d, member)),
            ).start()

        return carry

    lax.fori_loop(low, high, step, 0)


def rows_wait(place, source, target, send_sem, recv_sem, sign):
    own = place.slot(0, 0, 0)

    def step(i, carry):
        copy = pltpu.make_async_remote_copy(
            src_ref=source.at[i],
            dst_ref=target.at[i],
            send_sem=send_sem.at[i],
            recv_sem=recv_sem.at[i],
            device_id=place.device(y=1),
            device_id_type=MESH,
        )

        @pl.when(i != own)
        def _():
            copy.wait_send()
            copy.wait_recv()

        return carry

    lax.fori_loop(0, PEERS, step, 0)
    pltpu.make_async_copy(source.at[own], target.at[own], recv_sem.at[own]).wait()


def remote(source, target, send_sem, recv_sem, device):
    return pltpu.make_async_remote_copy(
        src_ref=source,
        dst_ref=target,
        send_sem=send_sem,
        recv_sem=recv_sem,
        device_id=device,
        device_id_type=MESH,
    )


def far_start(place, first, second, relay, send_sem, recv_sem):
    up = remote(
        first, relay.at[0], send_sem.at[0], recv_sem.at[0], place.device(z=HALF_Z // 2)
    )
    down = remote(
        second, relay.at[1], send_sem.at[1], recv_sem.at[1],
        place.device(c=1, z=-(HALF_Z // 2)),
    )
    up.start()
    down.start()
    return [up, down]


def far_relay(place, legs, relay, target_up, target_down, send_sem, recv_sem):
    up = remote(
        relay.at[0], target_up, send_sem.at[2], recv_sem.at[2], place.device(z=HALF_Z // 2)
    )
    down = remote(
        relay.at[1], target_down, send_sem.at[3], recv_sem.at[3],
        place.device(z=-(HALF_Z // 2)),
    )
    for leg, copy in zip(legs, (up, down)):
        leg.wait_recv()
        copy.start()
    return [up, down]


def ring_copy(place, source, target, send_sem, recv_sem, h, half, way, step):
    return remote(
        source, target, send_sem.at[h, half, way, step], recv_sem.at[h, half, way, step],
        place.device(y=1 - 2 * way),
    )


def dispatch_kernel(
    placement_ref, route_ref, x_hbm, g_hbm, weight_hbm, recv_ref, full_ref, target_ref,
    x_ref, g_ref, weight_ref, rows_ref, slice_ref, load_sem, relay, row_send, row_recv, far_send, far_recv, near_send, near_recv,
    ring_send, ring_recv, local_sem,
):
    place = Place()
    y, c = place.y, place.c
    loads = [
        pltpu.make_async_copy(source, into, load_sem.at[i])
        for i, (source, into) in enumerate(
            ((weight_hbm, weight_ref), (x_hbm, x_ref), (g_hbm, g_ref))
        )
    ]
    for load in loads:
        load.start()
    greet_all(place, 1)
    target = targets(place, placement_ref[...], route_ref[...])
    target_ref[...] = target
    slots, row_count = PEERS * 8, x_ref.shape[0]
    places = lax.broadcasted_iota(jnp.int32, (slots, row_count), 0) == target
    places = jnp.where(places, 1.0, 0.0).astype(jnp.bfloat16)
    loads[0].wait()
    slice_ref[...] = weight_ref[...].astype(jnp.bfloat16)
    loads[1].wait()
    hidden = x_ref.shape[1]
    rows_ref[:, :, :hidden] = (
        jnp.dot(places, x_ref[...], preferred_element_type=jnp.float32)
        .reshape(PEERS, 8, hidden)
        .astype(jnp.bfloat16)
    )
    loads[2].wait()
    for j in range(0, g_ref.shape[1], 512):
        rows_ref[:, :, hidden + j : hidden + j + 512] = (
            jnp.dot(places, g_ref[:, j : j + 512], preferred_element_type=jnp.float32)
            .reshape(PEERS, 8, 512)
            .astype(jnp.bfloat16)
        )
    wait_all()
    own = pltpu.make_async_copy(slice_ref.at[c], full_ref.at[0, y, c], local_sem)
    own.start()
    near = remote(
        slice_ref.at[1 - c], full_ref.at[0, y, c], near_send, near_recv, place.device(c=1)
    )
    near.start()
    legs = far_start(place, slice_ref.at[c], slice_ref.at[1 - c], relay, far_send, far_recv)
    rows_start(place, rows_ref, recv_ref, row_send, row_recv, 1, 0, FIRST_ROWS)
    sent = []

    def ring(h, step):
        for half in range(2):
            for way in range(2):
                if step >= HOPS - (half != way):
                    continue
                if step > 0:
                    sent[index[h, half, way]].wait_recv()
                origin = (y - (1 - 2 * way) * step + GRID_Y) % GRID_Y
                block = full_ref.at[h, origin, half]
                copy = ring_copy(place, block, block, ring_send, ring_recv, h, half, way, step)
                copy.start()
                index[h, half, way] = len(sent)
                sent.append(copy)

    index = {}
    own.wait()
    near.wait()
    ring(0, 0)
    ring(0, 1)
    more = far_relay(
        place, legs, relay, full_ref.at[1, y, c], full_ref.at[1, y, 1 - c], far_send, far_recv
    )
    rows_start(place, rows_ref, recv_ref, row_send, row_recv, 1, FIRST_ROWS, PEERS)
    ring(0, 2)
    for copy in more:
        copy.wait_recv()
    ring(1, 0)
    ring(0, 3)
    ring(1, 1)
    ring(1, 2)
    ring(1, 3)
    for i in index.values():
        sent[i].wait_recv()
    for copy in legs + more + sent:
        copy.wait_send()
    rows_wait(place, rows_ref, recv_ref, row_send, row_recv, 1)


def return_kernel(
    rows_ref, part_ref, home_ref, grad_ref,
    relay, hold, total, row_send, row_recv, far_send, far_recv, near_send, near_recv,
    ring_send, ring_recv, local_sem,
):
    place = Place()
    y, c = place.y, place.c
    greet_all(place, -1)
    wait_all()
    rows_start(place, rows_ref, home_ref, row_send, row_recv, -1, 0, FIRST_BACK)
    sent = []
    index = {}

    def ring(h, step):
        for half in range(2):
            for way in range(2):
                first = int(half != way)
                if step < first:
                    continue
                target = (y + (1 - 2 * way) * (HOPS - step) + GRID_Y) % GRID_Y
                if step == first:
                    source = part_ref.at[h, target, half]
                else:
                    sent[index[h, half, way]].wait_recv()
                    source = hold.at[h, way, step - 1, half]
                    source[...] = (
                        source[...].astype(jnp.float32)
                        + part_ref[h, target, half].astype(jnp.float32)
                    ).astype(jnp.bfloat16)
                copy = ring_copy(
                    place, source, hold.at[h, way, step, half],
                    ring_send, ring_recv, h, half, way, step,
                )
                copy.start()
                index[h, half, way] = len(sent)
                sent.append(copy)

    def finish(h):
        for half in range(2):
            for way in range(2):
                sent[index[h, half, way]].wait_recv()
        total[h] = (
            part_ref[h, y].astype(jnp.float32)
            + hold[h, 0, HOPS - 1].astype(jnp.float32)
            + hold[h, 1, HOPS - 1].astype(jnp.float32)
        ).astype(jnp.bfloat16)

    ring(1, 0)
    ring(1, 1)
    ring(1, 2)
    ring(0, 0)
    ring(1, 3)
    ring(0, 1)
    finish(1)
    legs = far_start(place, total.at[1, c], total.at[1, 1 - c], relay, far_send, far_recv)
    rows_start(place, rows_ref, home_ref, row_send, row_recv, -1, FIRST_BACK, PEERS)
    ring(0, 2)
    ring(0, 3)
    more = far_relay(
        place, legs, relay, grad_ref.at[c, 1], grad_ref.at[1 - c, 1], far_send, far_recv
    )
    finish(0)
    own = pltpu.make_async_copy(total.at[0, c], grad_ref.at[c, 0], local_sem)
    own.start()
    near = remote(
        total.at[0, 1 - c], grad_ref.at[c, 0], near_send, near_recv, place.device(c=1)
    )
    near.start()
    for copy in legs + sent:
        copy.wait_send()
    own.wait()
    near.wait()
    for copy in more:
        copy.wait()
    rows_wait(place, rows_ref, home_ref, row_send, row_recv, -1)


VMEM = pl.BlockSpec(memory_space=pltpu.VMEM)
DMA = pltpu.SemaphoreType.DMA


def dispatch(placement, route, x_rows, y_cot, master_weight):
    members, slice_rows, width = master_weight.shape
    row_count, hidden = x_rows.shape
    hbm = pl.BlockSpec(memory_space=pltpu.HBM)
    low = jnp.bfloat16
    return pl.pallas_call(
        dispatch_kernel,
        out_shape=(
            jax.ShapeDtypeStruct((PEERS, 8, hidden + width), low),
            jax.ShapeDtypeStruct((2, GRID_Y, 2, slice_rows, width), low),
            jax.ShapeDtypeStruct((1, row_count), jnp.int32),
        ),
        in_specs=[VMEM, VMEM, hbm, hbm, hbm],
        out_specs=(VMEM, VMEM, VMEM),
        scratch_shapes=[
            pltpu.VMEM(x_rows.shape, low),
            pltpu.VMEM(y_cot.shape, low),
            pltpu.VMEM(master_weight.shape, jnp.float32),
            pltpu.VMEM((PEERS, 8, hidden + width), low),
            pltpu.VMEM(master_weight.shape, low),
            DMA((3,)),
            pltpu.VMEM((2, slice_rows, width), low),
            DMA((PEERS,)), DMA((PEERS,)), DMA((4,)), DMA((4,)), DMA(()), DMA(()),
            DMA((2, 2, 2, HOPS)), DMA((2, 2, 2, HOPS)), DMA(()),
        ],
        compiler_params=pltpu.CompilerParams(
            collective_id=0, has_side_effects=True, vmem_limit_bytes=FIRST_LIMIT
        ),
        name="dispatch",
    )(
        *(
            pltpu.with_memory_space_constraint(array, pltpu.HBM)
            for array in (
                placement.reshape(1, -1), route.reshape(1, -1), x_rows, y_cot, master_weight
            )
        )
    )


def give_back(rows, part):
    slice_rows, width = part.shape[-2:]
    return pl.pallas_call(
        return_kernel,
        out_shape=(
            jax.ShapeDtypeStruct(rows.shape, rows.dtype),
            jax.ShapeDtypeStruct((2, 2, slice_rows, width), part.dtype),
        ),
        in_specs=[VMEM] * 2,
        out_specs=(VMEM, VMEM),
        scratch_shapes=[
            pltpu.VMEM((2, slice_rows, width), part.dtype),
            pltpu.VMEM((2, 2, HOPS, 2, slice_rows, width), part.dtype),
            pltpu.VMEM((2, 2, slice_rows, width), part.dtype),
            DMA((PEERS,)), DMA((PEERS,)), DMA((4,)), DMA((4,)), DMA(()), DMA(()),
            DMA((2, 2, 2, HOPS)), DMA((2, 2, 2, HOPS)), DMA(()),
        ],
        compiler_params=pltpu.CompilerParams(
            collective_id=1, has_side_effects=True, vmem_limit_bytes=VMEM_LIMIT
        ),
        name="give_back",
    )(rows, part)


def per_device(master_weight, m_code, m_scale, v_code, v_scale, placement, route, x_rows, y_cot):
    members, slice_rows, model_width = master_weight.shape
    row_count, hidden_width = x_rows.shape
    expert_count = placement.shape[0]
    groups = lax.axis_size("grp")
    replicas = lax.axis_size("rep")
    grad_factor = float(row_count * groups * replicas // expert_count) ** (-0.5)
    capacity = max(2, (3 * row_count + 2 * expert_count - 1) // (2 * expert_count))
    block_rows = 2 * capacity
    slots = PEERS * block_rows
    width = hidden_width + model_width
    recv, full, target = dispatch(placement, route, x_rows, y_cot, master_weight)
    places = (target.reshape(-1, 1) == lax.iota(jnp.int32, slots)[None, :]).astype(jnp.bfloat16)
    recv = recv.reshape(slots, width)
    half = lax.broadcasted_iota(jnp.int32, (slots, 1), 0) % block_rows // capacity
    local_x, local_g = recv[:, :hidden_width], recv[:, hidden_width:]
    wide_x = jnp.concatenate(
        [jnp.where(half == h, local_x, jnp.zeros_like(local_x)) for h in range(2)], axis=1
    )
    outer = lax.dot_general(
        wide_x, local_g, (((0,), (0,)), ((), ())), preferred_element_type=jnp.float32
    )
    part = (outer * grad_factor).astype(jnp.bfloat16)
    part = part.reshape(2, GRID_Y, 2, slice_rows, model_width)
    weight_flat = full.reshape(2 * hidden_width, model_width)
    y_total = jnp.dot(wide_x, weight_flat, preferred_element_type=jnp.float32)
    dx_wide = lax.dot_general(
        local_g, weight_flat, (((1,), (1,)), ((), ())), preferred_element_type=jnp.float32
    )
    dx_total = jnp.where(half == 0, dx_wide[:, :hidden_width], dx_wide[:, hidden_width:])
    back = jnp.concatenate([dx_total, y_total], axis=1).astype(jnp.bfloat16)
    home, grad_pairs = give_back(back.reshape(PEERS, block_rows, width), part)
    home = home.reshape(slots, width)
    y_rows = jnp.dot(places, home[:, hidden_width:], preferred_element_type=jnp.float32).astype(
        jnp.bfloat16
    )
    x_grad = jnp.dot(places, home[:, :hidden_width], preferred_element_type=jnp.float32).astype(
        jnp.bfloat16
    )
    return (y_rows, x_grad) + adam_update(master_weight, grad_pairs, m_code, m_scale, v_code, v_scale)


def solution(mesh):
    state = P("grp", "rep", None)
    rows = P(("rep", "grp"), None)
    return jax.shard_map(
        per_device,
        mesh=mesh,
        in_specs=(state, state, state, state, state, P(), P(("rep", "grp")), rows, rows),
        out_specs=(rows, rows, state, state, state, state, state),
        check_vma=False,
    )
```
